1024 devices in a mesh: pipe: 4 (over z_hi), dp: 64 (over x, y), tensor: 4 (over z_lo, core).
Axes of the slice: x: 8, y: 8, z: 8 (z_hi: 4, z_lo: 2; z = z_hi * 2 + z_lo), core: 2. Of those that a mesh axis runs over, the one named last changes fastest.
Arguments:
- up_weight: bfloat16 [4, 2048, 4096], P('pipe', None, 'tensor'), may hold values from -0.125 to 0.125
- down_weight: bfloat16 [4, 2048, 4096], P('pipe', None, 'tensor'), may hold values from -0.09375 to 0.09375
- gate_act: bfloat16 [4, 8192, 4096], P('pipe', 'dp', 'tensor'), may hold values from -0.27734375 to 2.5
- hidden: bfloat16 [4, 8192, 4096], P('pipe', 'dp', 'tensor'), may hold values from -6 to 6
- block_input: bfloat16 [4, 8192, 2048], P('pipe', ('dp', 'tensor')), may hold values from -6 to 6
- norm_gain: float32 [4, 2048], P('pipe'), may hold values from 0.1 to 1.9
- loss_grad: bfloat16 [8192, 2048], P(('dp', 'tensor')), may hold values from -2.5 to 2.5
- moment_one: float32 [4, 2048, 4096], P('pipe', 'dp', 'tensor'), may hold values from -6 to 6
- moment_two: float32 [4, 2048, 4096], P('pipe', 'dp', 'tensor'), may hold values from 1 to 30
Outputs:
- input_grad: bfloat16 [4, 8192, 2048], P('pipe', ('dp', 'tensor'))
- new_moment_one: float32 [4, 2048, 4096], P('pipe', 'dp', 'tensor')
- new_moment_two: float32 [4, 2048, 4096], P('pipe', 'dp', 'tensor')
- new_down_weight: float32 [4, 2048, 4096], P('pipe', 'dp', 'tensor')
The draws below stay inside these ranges and needn't reach their ends.
All inputs are finite; a program needn't handle non-finite values.
Results may differ from the reference program's by a relative error of at most 0.028.
Values may be sent and summed in bfloat16 or wider, within the bound.
A program may use at most 64 MiB of HBM per device.

```python
import math
import jax
import jax.numpy as jnp
from jax import lax

D = 2048
FF = 4096
TOK = 128
TOKENS = 8192
N_PIPE = 4
N_DP = 64
N_TENSOR = 4


def raised(drawn, stream_key, source, target, shards_of, factor):
    def block_of(axis_at):
        return (jnp.arange(drawn.shape[axis_at]) // (drawn.shape[axis_at] // shards_of)).reshape((-1,) + (1,) * (drawn.ndim - 1 - axis_at))

    one_side = jax.random.permutation(stream_key, shards_of)[block_of(target)]
    other_side = (block_of(target) + shards_of // 2) % shards_of
    return jnp.where((block_of(source) == one_side) | (block_of(source) == other_side), factor * drawn, drawn)


def shard_levels(stream_key, shape, pieces, smallest, largest):
    level, own = 1.0, jax.random.fold_in(stream_key, 6)
    for position, blocks in pieces:
        steps = jnp.exp(jax.random.uniform(jax.random.fold_in(own, position), (blocks,), jnp.float32, smallest / len(pieces), largest / len(pieces)))
        level = level * jnp.repeat(steps, shape[position] // blocks).reshape([-1 if axis == position else 1 for axis in range(len(shape))])
    return level


def noise(rng, extent, spread, most, split=(), held_as=jnp.bfloat16):
    drawn = spread * jax.random.normal(rng, extent, jnp.float32)
    if split:
        drawn = drawn * shard_levels(rng, extent, split, -0.22, 0.18)
    return jnp.clip(drawn, -most, most).astype(held_as)


def heavy_noise(stream_key, extent, scale, most, shards, heavy, held_as=jnp.bfloat16):
    entries = scale * jax.random.normal(stream_key, extent, jnp.float32)
    if shards:
        entries = entries * shard_levels(stream_key, extent, shards, -0.22, 0.18)
    return jnp.clip(raised(entries, jax.random.fold_in(stream_key, 3), *heavy), -most, most).astype(held_as)


def setup_inputs(seed: int = 0) -> dict:
    key_list = jax.random.split(jax.random.key(seed), 10)
    return {
        "up_weight": noise(key_list[0], (N_PIPE, D, FF), D ** -0.5, 0.125, ((0, 4), (2, 4))),
        "down_weight": noise(key_list[1], (N_PIPE, D, FF), FF ** -0.5, 0.09375, ((0, 4), (2, 4))),
        "gate_act": jnp.clip(-0.27734375 + 2.7773438 * jax.random.uniform(key_list[2], (N_PIPE, TOKENS, FF), jnp.float32) ** shard_levels(key_list[2], (N_PIPE, TOKENS, FF), ((0, 4), (1, 64), (2, 4)), -0.2, 0.2), -0.27734375, 2.5).astype(jnp.bfloat16),
        "hidden": noise(key_list[3], (N_PIPE, TOKENS, FF), 1.0, 6.0, ((0, 4), (1, 64), (2, 4))),
        "block_input": noise(key_list[4], (N_PIPE, TOKENS, D), 1.0, 6.0, ((0, 4), (1, 256))),
        "norm_gain": jnp.clip(1.0 + 0.18 * jax.random.normal(key_list[5], (N_PIPE, D), jnp.float32), 0.1, 1.9),
        "loss_grad": heavy_noise(key_list[6], (TOKENS, D), 0.1, 2.5, ((0, 256),), (0, 1, 256, 6.0)),
        "moment_one": noise(key_list[7], (N_PIPE, D, FF), 1.0, 6.0, ((0, 4), (1, 64), (2, 4)), jnp.float32),
        "moment_two": jnp.clip(jnp.exp(math.log(30.0) - 3.4011974 * jax.random.uniform(key_list[8], (N_PIPE, D, FF), jnp.float32) ** shard_levels(key_list[8], (N_PIPE, D, FF), ((0, 4), (1, 64), (2, 4)), -0.2, 0.2)), 1.0, 30.0),
    }


EPS_NORM = 1e-05
EPS_ADAM = 1e-08
BETA_ONE = 0.9
BETA_TWO = 0.95
RATE = 0.01
DECAY = 0.1
CORRECT_ONE = 1.0 - 0.9 ** 10
CORRECT_TWO = 1.0 - 0.95 ** 10

def rounded(value):
    return lax.optimization_barrier(value.astype(jnp.bfloat16)).astype(jnp.float32)

def reference(up_weight, down_weight, gate_act, hidden, block_input, norm_gain, loss_grad, moment_one, moment_two):
    upstream = loss_grad
    width = FF // N_TENSOR
    grads_out = []
    firsts = []
    seconds = []
    weights = []
    for layer in reversed(range(N_PIPE)):
        unit_grad = (jnp.dot(upstream, down_weight[layer], preferred_element_type=jnp.float32) * gate_act[layer].astype(jnp.float32)).astype(jnp.bfloat16)
        normed = jnp.zeros((TOKENS, D), jnp.float32)
        for block in range(N_TENSOR):
            left = unit_grad[:, block * width:(block + 1) * width]
            right = up_weight[layer][:, block * width:(block + 1) * width]
            term = lax.dot_general(left, right, (((1,), (1,)), ((), ())), preferred_element_type=jnp.float32)
            normed = normed + rounded(term)
        rows_in = block_input[layer].astype(jnp.float32)
        inverse_rms = lax.rsqrt(lax.optimization_barrier(jnp.mean(rows_in * rows_in, axis=-1, keepdims=True)) + EPS_NORM)
        scaled = normed * norm_gain[layer][None, :]
        mean_term = lax.optimization_barrier(jnp.mean(rows_in * scaled, axis=-1, keepdims=True))
        input_grad = (upstream.astype(jnp.float32) + inverse_rms * scaled - rows_in * inverse_rms ** 3 * mean_term).astype(jnp.bfloat16)
        upstream_blocks = upstream.reshape(N_DP, TOK, D)
        hidden_blocks = hidden[layer].reshape(N_DP, TOK, FF)

        def add_block(carry, pair):
            term = jnp.dot(pair[0].T, pair[1], preferred_element_type=jnp.float32)
            return (carry + rounded(term), None)
        gradient, _ = lax.scan(add_block, jnp.zeros((D, FF), jnp.float32), (upstream_blocks, hidden_blocks))
        first = BETA_ONE * moment_one[layer] + (1.0 - BETA_ONE) * gradient
        second = BETA_TWO * moment_two[layer] + (1.0 - BETA_TWO) * gradient * gradient
        current = down_weight[layer].astype(jnp.float32)
        direction = first / CORRECT_ONE / (jnp.sqrt(second / CORRECT_TWO) + EPS_ADAM) + DECAY * current
        grads_out.append(input_grad)
        firsts.append(first)
        seconds.append(second)
        weights.append(current - RATE * direction)
        upstream = input_grad
    grads_out = grads_out[::-1]
    firsts = firsts[::-1]
    seconds = seconds[::-1]
    weights = weights[::-1]
    return (jnp.stack(grads_out), jnp.stack(firsts), jnp.stack(seconds), jnp.stack(weights))
```

```python
import functools

import jax
import jax.numpy as jnp
from jax import lax
from jax.experimental import pallas as pl
from jax.experimental.pallas import tpu as pltpu
from jax.sharding import PartitionSpec as P

EPS_NORM = 1e-05
EPS_ADAM = 1e-08
BETA_ONE = 0.9
BETA_TWO = 0.95
RATE = 0.01
DECAY = 0.1
CORRECT_ONE = 1.0 - 0.9**10
CORRECT_TWO = 1.0 - 0.95**10

MESH = pl.DeviceIdType.MESH
F32 = jnp.float32
BF16 = jnp.bfloat16


def kernel(
    grid_x, grid_y, chunks,
    w_up, w_down, gate_act, hidden, block_input, norm_gain, loss_grad, moment_one, moment_two,
    out_dx, out_first, out_second, out_weight,
    wd, wu, gates, rows_in, gain, mom1, mom2,
    up, up_t, acc, unit, part, half_send, half_recv, quarter_send, quarter_recv, scaled, dx,
    hid_a, hid_b, upt_a, upt_b, grad_a, grad_b, gsend_a, gsend_b, grecv_a, grecv_b,
    first_v, second_v, weight_v,
    sem_in, sem_out, sem_block, sem_mate, sem_half, sem_quarter,
    sem_hid_a, sem_hid_b, sem_upt_a, sem_upt_b, sem_mate_a, sem_mate_b, sem_grad_a, sem_grad_b,
    send_fwd, send_mate, send_half, send_quarter, send_dx,
    send_hid, send_upt, send_upt_mate, send_grad,
):
    pipe = lax.axis_index("pipe")
    owner = lax.axis_index("dp")
    tensor = lax.axis_index("tensor")
    sections = lax.axis_size("pipe")
    x = lax.div(owner, grid_y)
    y = lax.rem(owner, grid_y)
    chip = lax.div(tensor, 2)
    core = lax.rem(tensor, 2)
    mate = {"tensor": chip * 2 + 1 - core}
    across = {"tensor": (1 - chip) * 2 + core}
    last = pipe == sections - 1
    tokens, width = up.shape
    share = tokens // 4
    units = wd.shape[1]
    row_share = width // (grid_x * grid_y)
    span = width // chunks
    cols = units // 2

    def x_peer(k):
        return lax.rem(x + k, grid_x)

    def y_peer(k):
        return lax.rem(y + k, grid_y)

    def aligned(value, step):
        return pl.multiple_of(value * step, step)

    def remote(src, dst, send, recv, device):
        return pltpu.make_async_remote_copy(
            src_ref=src, dst_ref=dst, send_sem=send, recv_sem=recv, device_id=device, device_id_type=MESH
        )

    sent = []

    def start(copy, when=None):
        if when is None:
            copy.start()
        else:
            pl.when(when)(copy.start)
        sent.append((copy, when))

    order = [(0, 0), (0, 1), (1, 0), (1, 1)]

    def token_rows(c, z):
        return pl.ds((z * 2 + c) * share, share)

    loads = {}

    def load(name, src, dst, when=None):
        copy = pltpu.make_async_copy(src, dst, sem_in.at[len(loads)])
        loads[name] = copy
        if when is None:
            copy.start()
        else:
            pl.when(when)(copy.start)

    my_rows = pl.ds(aligned(core * 2 + chip, share), share)
    load("loss", loss_grad, up.at[my_rows], last)
    load("wd", w_down.at[0], wd)
    load("rows", block_input.at[0], rows_in)
    load("gain", norm_gain, gain)
    for n, (c, z) in enumerate(order):
        load(f"gate{n}", gate_act.at[0, token_rows(c, z)], gates.at[pl.ds(n * share, share)])
    load("wu", w_up.at[0], wu)
    for n, (c, z) in enumerate(order):
        src = hidden.at[0, token_rows(c, z)]
        load(f"hida{n}", src.at[:, pl.ds(0, cols)], hid_a.at[x, pl.ds(n * share, share)])
        load(f"hidb{n}", src.at[:, pl.ds(cols, cols)], hid_b.at[y, pl.ds(n * share, share)])
    load("mom1", moment_one.at[0], mom1)
    load("mom2", moment_two.at[0], mom2)

    barrier = pltpu.get_barrier_semaphore()

    def greet(device):
        pl.semaphore_signal(barrier, inc=1, device_id=device, device_id_type=MESH)

    greet(mate)
    greet(across)

    @pl.when(jnp.logical_and(pipe < sections - 1, chip == 1))
    def _():
        greet({"pipe": pipe + 1, "tensor": core})
        greet({"pipe": pipe + 1, "tensor": 2 + core})

    for k in range(1, grid_x):
        greet({"dp": x_peer(k) * grid_y + y})
    for k in range(1, grid_y):
        greet({"dp": x * grid_y + y_peer(k)})

    @pl.when(pipe == 0)
    def _():
        pl.semaphore_wait(barrier, grid_x + grid_y)

    @pl.when(pipe > 0)
    def _():
        pl.semaphore_wait(barrier, grid_x + grid_y + 1)

    pl.when(last)(loads["loss"].wait)

    def columns(j):
        return pl.ds(j * span, span)

    def block(z, c, j):
        return up.at[pl.ds(aligned(c * 2 + z, share), share), columns(j)]

    for z in range(2):
        for j in range(chunks):
            ref = block(z, core, j)
            start(
                remote(ref, ref, send_fwd.at[z, j], sem_block.at[z, j], across),
                jnp.logical_and(last, chip == z),
            )
            sent.pop()

    for n in range(4):
        loads[f"hida{n}"].wait()
        loads[f"hidb{n}"].wait()
    for k in range(1, grid_x):
        ref = hid_a.at[x]
        start(remote(ref, ref, send_hid.at[k], sem_hid_a.at[x], {"dp": x_peer(k) * grid_y + y}))
    for k in range(1, grid_y):
        ref = hid_b.at[y]
        start(remote(ref, ref, send_hid.at[grid_x + k], sem_hid_b.at[y], {"dp": x * grid_y + y_peer(k)}))

    for name in ("wd", "rows", "gain", "wu", "mom1", "mom2"):
        loads[name].wait()
    for n in range(4):
        loads[f"gate{n}"].wait()

    source = rows_in[...].astype(F32)
    inverse_rms = lax.rsqrt(jnp.mean(source * source, axis=-1, keepdims=True) + EPS_NORM)

    def pass_on(j):
        for z in range(2):
            ref = block(z, core, j)
            forward = remote(ref, ref, send_fwd.at[z, j], sem_block.at[z, j], across)
            own = jnp.logical_and(last, chip == z)
            pl.when(jnp.logical_not(own))(forward.wait_recv)
            relay = jnp.logical_and(jnp.logical_not(last), chip == 1)
            pl.when(relay)(forward.start)
            sent.append((forward, jnp.logical_or(own, relay)))
            start(remote(ref, ref, send_mate.at[z, j], sem_mate.at[z, j], mate))

    def multiply(j):
        for z in range(2):
            ref = block(z, 1 - core, j)
            remote(ref, ref, send_mate.at[z, j], sem_mate.at[z, j], mate).wait_recv()
        left = up[:, columns(j)]
        for n in range(0, units, 256):
            right = pl.ds(n, 256)
            term = jnp.dot(left, wd[columns(j), right], preferred_element_type=F32)
            if j > 0:
                term = term + acc[:, right]
            if j < chunks - 1:
                acc[:, right] = term
            else:
                unit[:, right] = (term * gates[:, right].astype(F32)).astype(BF16)

    per = grid_x // chunks

    def turn(j):
        turned = up[:, columns(j)].astype(F32).T.astype(BF16)
        up_t[pl.ds(j * per, per)] = turned.reshape(per, grid_y, row_share, tokens)

    pass_on(0)
    for j in range(chunks):
        if j + 1 < chunks:
            pass_on(j + 1)
        multiply(j)
        if j + 1 < chunks:
            turn(j)

    mates_half = pl.ds(aligned(1 - core, 2 * share), 2 * share)
    far = pl.ds(aligned(core * 2 + 1 - chip, share), share)
    far_half = pl.ds(aligned(1 - chip, share), share)
    near_half = pl.ds(aligned(chip, share), share)

    def second(i):
        for n in range(i * span, (i + 1) * span, 256):
            part[:, pl.ds(n, 256)] = lax.dot_general(
                unit[...], wu[pl.ds(n, 256), :], (((1,), (1,)), ((), ())), preferred_element_type=F32
            )
        half_send[:, columns(i)] = part[mates_half, columns(i)].astype(BF16)
        start(
            remote(
                half_send.at[:, columns(i)], half_recv.at[:, columns(i)], send_half.at[i], sem_half.at[i], mate
            )
        )

    def chip_sum(i):
        got = half_recv.at[:, columns(i)]
        remote(got, got, send_half.at[i], sem_half.at[i], mate).wait_recv()
        quarter_send[:, columns(i)] = (
            part[far, columns(i)] + half_recv[far_half, columns(i)].astype(F32)
        ).astype(BF16)
        start(
            remote(
                quarter_send.at[:, columns(i)],
                quarter_recv.at[:, columns(i)],
                send_quarter.at[i],
                sem_quarter.at[i],
                across,
            )
        )

    second(0)
    turn(chunks - 1)

    half_y, half_x = grid_y // 2, grid_x // 2
    for k in range(1, grid_x):
        start(
            remote(
                up_t.at[x_peer(k), pl.ds(core * half_y, half_y)],
                upt_a.at[pl.ds(core * half_y, half_y), :, pl.ds(aligned(x, tokens), tokens)],
                send_upt.at[k],
                sem_upt_a.at[x],
                {"dp": x_peer(k) * grid_y + y},
            )
        )
    for k in range(1, grid_y):
        start(
            remote(
                up_t.at[pl.ds(core * half_x, half_x), y_peer(k)],
                upt_b.at[pl.ds(core * half_x, half_x), :, pl.ds(aligned(y, tokens), tokens)],
                send_upt.at[grid_x + k],
                sem_upt_b.at[y],
                {"dp": x * grid_y + y_peer(k)},
            )
        )

    for i in range(1, chunks):
        second(i)
        chip_sum(i - 1)
    chip_sum(chunks - 1)

    total = jnp.zeros((share, 1), F32)
    for i in range(chunks):
        got = quarter_recv.at[:, columns(i)]
        remote(got, got, send_quarter.at[i], sem_quarter.at[i], across).wait_recv()
        normed = (
            part[my_rows, columns(i)]
            + half_recv[near_half, columns(i)].astype(F32)
            + quarter_recv[:, columns(i)].astype(F32)
        )
        value = normed * gain[:, columns(i)]
        scaled[:, columns(i)] = value
        total = total + jnp.sum(rows_in[:, columns(i)].astype(F32) * value, axis=-1, keepdims=True)
    slope = inverse_rms * inverse_rms * inverse_rms * (total / width)
    for i in range(chunks):
        dx[:, columns(i)] = (
            up[my_rows, columns(i)].astype(F32)
            + inverse_rms * scaled[:, columns(i)]
            - rows_in[:, columns(i)].astype(F32) * slope
        ).astype(BF16)
        start(
            remote(
                dx.at[:, columns(i)],
                up.at[my_rows, columns(i)],
                send_dx.at[i],
                sem_block.at[chip, i],
                {"pipe": jnp.maximum(pipe - 1, 0), "tensor": 2 + core},
            ),
            pipe > 0,
        )
    outs = [pltpu.make_async_copy(dx, out_dx.at[0], sem_out.at[0])]
    outs[0].start()

    upt_a[:, :, pl.ds(aligned(x, tokens), tokens)] = up_t[x]
    upt_b[:, :, pl.ds(aligned(y, tokens), tokens)] = up_t[:, y]

    def collect(slots, sem, mate_sem, send, half, me, size):
        here = pl.ds(core * half, half)
        there = pl.ds((1 - core) * half, half)
        for k in range(size - 1, 0, -1):
            other = lax.rem(me + k, size)
            lane = pl.ds(aligned(other, tokens), tokens)
            mine = slots.at[here, :, lane]
            copy = remote(mine, mine, send.at[k], sem.at[other], mate)
            copy.wait_recv()
            start(remote(mine, mine, send.at[k], mate_sem.at[other], mate))
        for k in range(size - 1, 0, -1):
            other = lax.rem(me + k, size)
            lane = pl.ds(aligned(other, tokens), tokens)
            theirs = slots.at[there, :, lane]
            remote(theirs, theirs, send.at[k], mate_sem.at[other], mate).wait_recv()

    def gather_wait(slots, sem, me, size):
        for k in range(1, size):
            other = lax.rem(me + k, size)
            got = slots.at[other]
            remote(got, got, send_hid.at[k], sem.at[other], mate).wait_recv()

    def contract(slots, hid, grad, gsend, size):
        left = slots[...].reshape(size * row_share, slots.shape[2])
        right = hid[...].reshape(hid.shape[0] * tokens, cols)
        for n in range(0, cols, 256):
            wide = min(256, cols)
            term = jnp.dot(left, right[:, n : n + wide], preferred_element_type=F32)
            term = term.reshape(size, row_share, wide)
            grad[:, :, pl.ds(n, wide)] = term
            gsend[:, :, pl.ds(n, wide)] = term.astype(BF16)

    gather_wait(hid_a, sem_hid_a, x, grid_x)
    collect(upt_a, sem_upt_a, sem_mate_a, send_upt_mate.at[0], half_y, x, grid_x)
    contract(upt_a, hid_a, grad_a, gsend_a, grid_y)
    for k in range(1, grid_y):
        start(
            remote(
                gsend_a.at[y_peer(k)], grecv_a.at[y], send_grad.at[k], sem_grad_a.at[y],
                {"dp": x * grid_y + y_peer(k)},
            )
        )
    gather_wait(hid_b, sem_hid_b, y, grid_y)
    collect(upt_b, sem_upt_b, sem_mate_b, send_upt_mate.at[1], half_x, y, grid_y)
    contract(upt_b, hid_b, grad_b, gsend_b, grid_x)
    for k in range(1, grid_x):
        start(
            remote(
                gsend_b.at[x_peer(k)], grecv_b.at[x], send_grad.at[grid_y + k], sem_grad_b.at[x],
                {"dp": x_peer(k) * grid_y + y},
            )
        )

    def update(grad, grecv, sem, me, size, offset):
        gradient = grad[me]
        for k in range(size - 1, 0, -1):
            other = lax.rem(me + k, size)
            got = grecv.at[other]
            remote(got, got, send_grad.at[k], sem.at[other], mate).wait_recv()
            gradient = gradient + grecv[other].astype(F32)
        at = pl.ds(offset, cols)
        current = wd[pl.ds(aligned(owner, row_share), row_share), at].astype(F32)
        one = BETA_ONE * mom1[:, at] + (1.0 - BETA_ONE) * gradient
        two = BETA_TWO * mom2[:, at] + (1.0 - BETA_TWO) * gradient * gradient
        direction = one / CORRECT_ONE / (jnp.sqrt(two / CORRECT_TWO) + EPS_ADAM) + DECAY * current
        first_v[:, at] = one
        second_v[:, at] = two
        weight_v[:, at] = current - RATE * direction

    update(grad_a, grecv_a, sem_grad_a, y, grid_y, 0)
    update(grad_b, grecv_b, sem_grad_b, x, grid_x, cols)
    for n, (value, out) in enumerate(((first_v, out_first), (second_v, out_second), (weight_v, out_weight))):
        copy = pltpu.make_async_copy(value, out.at[0], sem_out.at[1 + n])
        copy.start()
        outs.append(copy)
    for copy in outs:
        copy.wait()
    for copy, when in sent:
        if when is None:
            copy.wait_send()
        else:
            pl.when(when)(copy.wait_send)


def on_device(grid_x, grid_y, chunks, *args):
    w_up, w_down, gate_act, hidden, block_input, norm_gain, loss_grad, moment_one, moment_two = args
    width, units = w_up.shape[1:]
    tokens = gate_act.shape[1]
    share = tokens // 4
    cols = units // 2
    row_share = width // (grid_x * grid_y)
    outs = [
        jax.ShapeDtypeStruct(block_input.shape, BF16),
        *[jax.ShapeDtypeStruct(moment_one.shape, F32) for _ in range(3)],
    ]
    dma = pltpu.SemaphoreType.DMA
    vmem = pltpu.VMEM
    scratch = [
        vmem((width, units), BF16),
        vmem((width, units), BF16),
        vmem((tokens, units), BF16),
        vmem((share, width), BF16),
        vmem((1, width), F32),
        vmem((row_share, units), F32),
        vmem((row_share, units), F32),
        vmem((tokens, width), BF16),
        vmem((grid_x, grid_y, row_share, tokens), BF16),
        vmem((tokens, units), F32),
        vmem((tokens, units), BF16),
        vmem((tokens, width), F32),
        vmem((2 * share, width), BF16),
        vmem((2 * share, width), BF16),
        vmem((share, width), BF16),
        vmem((share, width), BF16),
        vmem((share, width), F32),
        vmem((share, width), BF16),
        vmem((grid_x, tokens, cols), BF16),
        vmem((grid_y, tokens, cols), BF16),
        vmem((grid_y, row_share, grid_x * tokens), BF16),
        vmem((grid_x, row_share, grid_y * tokens), BF16),
        vmem((grid_y, row_share, cols), F32),
        vmem((grid_x, row_share, cols), F32),
        vmem((grid_y, row_share, cols), BF16),
        vmem((grid_x, row_share, cols), BF16),
        vmem((grid_y, row_share, cols), BF16),
        vmem((grid_x, row_share, cols), BF16),
        vmem((row_share, units), F32),
        vmem((row_share, units), F32),
        vmem((row_share, units), F32),
        dma((24,)),
        dma((4,)),
        dma((2, chunks)),
        dma((2, chunks)),
        dma((chunks,)),
        dma((chunks,)),
        dma((grid_x,)),
        dma((grid_y,)),
        dma((grid_x,)),
        dma((grid_y,)),
        dma((grid_x,)),
        dma((grid_y,)),
        dma((grid_y,)),
        dma((grid_x,)),
        dma((2, chunks)),
        dma((2, chunks)),
        dma((chunks,)),
        dma((chunks,)),
        dma((chunks,)),
        dma((grid_x + grid_y,)),
        dma((grid_x + grid_y,)),
        dma((2, max(grid_x, grid_y))),
        dma((grid_x + grid_y,)),
    ]
    anywhere = pl.BlockSpec(memory_space=pl.ANY)
    return pl.pallas_call(
        functools.partial(kernel, grid_x, grid_y, chunks),
        out_shape=outs,
        in_specs=[anywhere] * 9,
        out_specs=[anywhere] * 4,
        scratch_shapes=scratch,
        compiler_params=pltpu.CompilerParams(
            collective_id=0, has_side_effects=True, vmem_limit_bytes=67043328
        ),
    )(*args)


def solution(mesh, grid=(8, 8), chunks=4):
    in_specs = (
        P("pipe", None, "tensor"),
        P("pipe", None, "tensor"),
        P("pipe", "dp", "tensor"),
        P("pipe", "dp", "tensor"),
        P("pipe", ("dp", "tensor"), None),
        P("pipe", None),
        P(("dp", "tensor"), None),
        P("pipe", "dp", "tensor"),
        P("pipe", "dp", "tensor"),
    )
    out_specs = (
        P("pipe", ("dp", "tensor"), None),
        P("pipe", "dp", "tensor"),
        P("pipe", "dp", "tensor"),
        P("pipe", "dp", "tensor"),
    )
    return jax.shard_map(
        functools.partial(on_device, *grid, chunks),
        mesh=mesh, in_specs=in_specs, out_specs=out_specs, check_vma=False,
    )
```

```python
import functools

import jax
import jax.numpy as jnp
from jax import lax
from jax.experimental import pallas as pl
from jax.experimental.pallas import tpu as pltpu
from jax.sharding import PartitionSpec as P

EPS_NORM = 1e-05
EPS_ADAM = 1e-08
BETA_ONE = 0.9
BETA_TWO = 0.95
RATE = 0.01
DECAY = 0.1
CORRECT_ONE = 1.0 - 0.9**10
CORRECT_TWO = 1.0 - 0.95**10

MESH = pl.DeviceIdType.MESH
F32 = jnp.float32
BF16 = jnp.bfloat16


def far_first(size):
    return sorted(range(1, size), key=lambda k: -min(k, size - k))


def kernel(
    grid_x, grid_y, chunks,
    w_up, w_down, gate_act, hidden, block_input, norm_gain, loss_grad,
    out_dx, out_grad,
    wd, wu, gates, rows_in, gain,
    up, up_t, acc, unit, part, block_send, block_recv, scaled, dx,
    hid_a, hid_b, upt_a, upt_b, grad_a, grad_b, gsend_a, gsend_b, grecv_a, grecv_b, gradient,
    sem_in, sem_out, sem_block, sem_mate, sem_sum,
    sem_hid_a, sem_hid_b, sem_upt_a, sem_upt_b, sem_mate_a, sem_mate_b, sem_grad_a, sem_grad_b,
    send_fwd, send_mate, send_sum, send_dx,
    send_hid, send_upt, send_upt_mate, send_grad,
):
    pipe = lax.axis_index("pipe")
    owner = lax.axis_index("dp")
    tensor = lax.axis_index("tensor")
    sections = lax.axis_size("pipe")
    x = lax.div(owner, grid_y)
    y = lax.rem(owner, grid_y)
    chip = lax.div(tensor, 2)
    core = lax.rem(tensor, 2)
    mate = {"tensor": chip * 2 + 1 - core}
    across = {"tensor": (1 - chip) * 2 + core}
    last = pipe == sections - 1
    streams, stream, width = up.shape
    tokens = streams * stream
    share = tokens // 4
    sub = stream // 4
    units = wd.shape[1]
    row_share = width // (grid_x * grid_y)
    span = width // chunks
    cols = units // 2

    def x_peer(k):
        return lax.rem(x + k, grid_x)

    def y_peer(k):
        return lax.rem(y + k, grid_y)

    def at_x(index):
        return {"dp": index * grid_y + y}

    def at_y(index):
        return {"dp": x * grid_y + index}

    def aligned(value, step):
        return pl.multiple_of(value * step, step)

    def remote(src, dst, send, recv, device):
        return pltpu.make_async_remote_copy(
            src_ref=src, dst_ref=dst, send_sem=send, recv_sem=recv, device_id=device, device_id_type=MESH
        )

    sent = []
    targets = (1,)

    def start(copy, when=None):
        if when is None:
            copy.start()
        else:
            pl.when(when)(copy.start)
        sent.append((copy, when))

    order = [(s, c, z) for s in range(streams) for c in range(2) for z in range(2)]

    def token_rows(s, c, z):
        return pl.ds((z * 2 + c) * share + s * sub, sub)

    def stream_rows(s):
        return pl.ds(s * sub, sub)

    def columns(j):
        return pl.ds(j * span, span)

    loads = {}

    def load(name, src, dst, when=None):
        copy = pltpu.make_async_copy(src, dst, sem_in.at[len(loads)])
        loads[name] = copy
        if when is None:
            copy.start()
        else:
            pl.when(when)(copy.start)

    my_rows = pl.ds(aligned(core * 2 + chip, sub), sub)
    for s in range(streams):
        load(f"loss{s}", loss_grad.at[stream_rows(s)], up.at[s, my_rows], last)
    load("wd", w_down.at[0], wd)
    load("rows", block_input.at[0], rows_in)
    load("gain", norm_gain, gain)
    for n, key in enumerate(order):
        load(f"gate{n}", gate_act.at[0, token_rows(*key)], gates.at[pl.ds(n * sub, sub)])
    load("wu", w_up.at[0], wu)
    for n, key in enumerate(order):
        src = hidden.at[0, token_rows(*key)]
        load(f"hida{n}", src.at[:, pl.ds(0, cols)], hid_a.at[x, pl.ds(n * sub, sub)])
        load(f"hidb{n}", src.at[:, pl.ds(cols, cols)], hid_b.at[y, pl.ds(n * sub, sub)])

    others = [
        (across, core * 2 + 1 - chip),
        ({"tensor": (1 - chip) * 2 + 1 - core}, (1 - core) * 2 + 1 - chip),
        (mate, (1 - core) * 2 + chip),
    ]

    barrier = pltpu.get_barrier_semaphore()

    def greet(device):
        pl.semaphore_signal(barrier, inc=1, device_id=device, device_id_type=MESH)

    for k in far_first(grid_x):
        greet(at_x(x_peer(k)))
    for k in far_first(grid_y):
        greet(at_y(y_peer(k)))

    @pl.when(jnp.logical_and(pipe < sections - 1, chip == 1))
    def _():
        greet({"pipe": pipe + 1, "tensor": core})
        greet({"pipe": pipe + 1, "tensor": 2 + core})

    for device, _ in others:
        greet(device)

    @pl.when(pipe == 0)
    def _():
        pl.semaphore_wait(barrier, grid_x + grid_y + 1)

    @pl.when(pipe > 0)
    def _():
        pl.semaphore_wait(barrier, grid_x + grid_y + 2)

    @pl.when(last)
    def _():
        for s in range(streams):
            for j in range(chunks):
                remote(
                    loss_grad.at[stream_rows(s), columns(j)], up.at[s, my_rows, columns(j)],
                    send_fwd.at[s, chip, j], sem_block.at[s, chip, j], across,
                ).start()
        for s in range(streams):
            loads[f"loss{s}"].wait()

    for n in range(len(order)):
        loads[f"hida{n}"].wait()
        loads[f"hidb{n}"].wait()
    for k in far_first(grid_x):
        ref = hid_a.at[x]
        start(remote(ref, ref, send_hid.at[k], sem_hid_a.at[x], at_x(x_peer(k))))
    for k in far_first(grid_y):
        ref = hid_b.at[y]
        start(remote(ref, ref, send_hid.at[grid_x + k], sem_hid_b.at[y], at_y(y_peer(k))))

    loads["rows"].wait()
    source = rows_in[...].astype(F32)
    inverse_rms = lax.rsqrt(jnp.mean(source * source, axis=-1, keepdims=True) + EPS_NORM)
    for name in ("wd", "gain", "wu"):
        loads[name].wait()
    for n in range(len(order)):
        loads[f"gate{n}"].wait()

    def block(s, z, c, j):
        return up.at[s, pl.ds(aligned(c * 2 + z, sub), sub), columns(j)]

    def pass_on(s, j):
        for z in range(2):
            ref = block(s, z, core, j)
            forward = remote(ref, ref, send_fwd.at[s, z, j], sem_block.at[s, z, j], across)
            own = jnp.logical_and(last, chip == z)
            pl.when(jnp.logical_not(own))(forward.wait_recv)
            relay = jnp.logical_and(jnp.logical_not(last), chip == 1)
            pl.when(relay)(forward.start)
            sent.append((forward, jnp.logical_or(own, relay)))
            start(remote(ref, ref, send_mate.at[s, z, j], sem_mate.at[s, z, j], mate))

    def multiply(s, j):
        for z in range(2):
            ref = block(s, z, 1 - core, j)
            remote(ref, ref, send_mate.at[s, z, j], sem_mate.at[s, z, j], mate).wait_recv()
        left = up[s, :, columns(j)]
        for n in range(0, units, 256):
            right = pl.ds(n, 256)
            term = jnp.dot(left, wd[columns(j), right], preferred_element_type=F32)
            if j > 0:
                term = term + acc[:, right]
            if j < chunks - 1:
                acc[:, right] = term
            else:
                unit[:, right] = (term * gates[pl.ds(s * stream, stream), right].astype(F32)).astype(BF16)

    def sums(s, i):
        return [
            remote(
                block_send.at[s, pl.ds(aligned(row, sub), sub), columns(i)], block_recv.at[s, n, :, columns(i)],
                send_sum.at[s, n, i], sem_sum.at[s, n, i], device,
            )
            for n, (device, row) in enumerate(others)
        ]

    def second(s, i):
        for n in range(i * span, (i + 1) * span, 256):
            term = lax.dot_general(
                unit[...], wu[pl.ds(n, 256), :], (((1,), (1,)), ((), ())), preferred_element_type=F32
            )
            part[s, :, pl.ds(n, 256)] = term
            block_send[s, :, pl.ds(n, 256)] = term.astype(BF16)
        for copy in sums(s, i):
            start(copy)

    def finish(s):
        rows = stream_rows(s)
        scale = inverse_rms[s * sub : (s + 1) * sub]
        total = jnp.zeros((sub, 1), F32)
        for i in range(chunks):
            normed = part[s, my_rows, columns(i)]
            for n, copy in reversed(list(enumerate(sums(s, i)))):
                copy.wait_recv()
                normed = normed + block_recv[s, n, :, columns(i)].astype(F32)
            value = normed * gain[:, columns(i)]
            scaled[:, columns(i)] = value
            total = total + jnp.sum(rows_in[rows, columns(i)].astype(F32) * value, axis=-1, keepdims=True)
        slope = scale * scale * scale * (total / width)
        for i in range(chunks):
            dx[rows, columns(i)] = (
                up[s, my_rows, columns(i)].astype(F32)
                + scale * scaled[:, columns(i)]
                - rows_in[rows, columns(i)].astype(F32) * slope
            ).astype(BF16)
            for z in targets:
                start(
                    remote(
                        dx.at[rows, columns(i)], up.at[s, my_rows, columns(i)],
                        send_dx.at[s, z, i], sem_block.at[s, chip, i],
                        {"pipe": jnp.maximum(pipe - 1, 0), "tensor": z * 2 + core},
                    ),
                    pipe > 0,
                )

    half_y, half_x = grid_y // 2, grid_x // 2
    my_x, my_y = pl.ds(aligned(x, tokens), tokens), pl.ds(aligned(y, tokens), tokens)
    y_half, x_half = pl.ds(core * half_y, half_y), pl.ds(core * half_x, half_x)
    spread_a = [
        remote(
            up_t.at[x_peer(k), y_half], upt_a.at[y_half, :, my_x], send_upt.at[k], sem_upt_a.at[x], at_x(x_peer(k))
        )
        for k in far_first(grid_x)
    ]
    spread_b = [
        remote(
            up_t.at[x_half, y_peer(k)], upt_b.at[x_half, :, my_y], send_upt.at[grid_x + k], sem_upt_b.at[y],
            at_y(y_peer(k)),
        )
        for k in far_first(grid_y)
    ]

    def spread():
        per = grid_x // 4
        for j in range(4):
            wide = pl.ds(j * (width // 4), width // 4)
            turned = up[:, :, wide].reshape(tokens, width // 4).astype(F32).T.astype(BF16)
            if per:
                up_t[pl.ds(j * per, per)] = turned.reshape(per, grid_y, row_share, tokens)
            else:
                up_t[j // 2, pl.ds((j % 2) * half_y, half_y)] = turned.reshape(half_y, row_share, tokens)
        for n in range(max(grid_x, grid_y) - 1):
            for copies in (spread_a, spread_b):
                if n < len(copies):
                    copies[n].start()
        upt_a[:, :, my_x] = up_t[x]
        upt_b[:, :, my_y] = up_t[:, y]

    for s in range(streams):
        pass_on(s, 0)
        for j in range(chunks):
            if j + 1 < chunks:
                pass_on(s, j + 1)
            multiply(s, j)
        if s == streams - 1:
            pl.when(pipe == 0)(spread)
        for i in range(chunks):
            second(s, i)
        if s > 0:
            finish(s - 1)
    finish(streams - 1)
    outs = [pltpu.make_async_copy(dx, out_dx.at[0], sem_out.at[0])]
    outs[0].start()
    pl.when(pipe > 0)(spread)
    sent.extend((copy, None) for copy in spread_a + spread_b)

    def arrivals(me, size):
        return [lax.rem(me + size - k, size) for k in far_first(size)]

    def lane(slots, part_of, other):
        return slots.at[part_of, :, pl.ds(aligned(other, tokens), tokens)]

    def share_one(slots, mine, sem, mate_sem, send, n, other):
        ref = lane(slots, mine, other)
        copy = remote(ref, ref, send.at[n], sem.at[other], mate)
        copy.wait_recv()
        start(remote(ref, ref, send.at[n], mate_sem.at[other], mate))

    def shared(slots, theirs, mate_sem, send, me, size):
        for n, other in enumerate(arrivals(me, size)):
            ref = lane(slots, theirs, other)
            remote(ref, ref, send.at[n], mate_sem.at[other], mate).wait_recv()

    def gather_wait(slots, sem, me, size):
        for other in arrivals(me, size):
            got = slots.at[other]
            remote(got, got, send_hid.at[0], sem.at[other], mate).wait_recv()

    def contract(slots, hid, grad, gsend, size):
        left = slots[...].reshape(size * row_share, slots.shape[2])
        right = hid[...].reshape(hid.shape[0] * tokens, cols)
        for n in range(0, cols, 256):
            wide = min(256, cols)
            term = jnp.dot(left, right[:, n : n + wide], preferred_element_type=F32)
            term = term.reshape(size, row_share, wide)
            grad[:, :, pl.ds(n, wide)] = term
            gsend[:, :, pl.ds(n, wide)] = term.astype(BF16)

    gather_wait(hid_a, sem_hid_a, x, grid_x)
    gather_wait(hid_b, sem_hid_b, y, grid_y)
    from_x, from_y = arrivals(x, grid_x), arrivals(y, grid_y)
    for n in range(max(len(from_x), len(from_y))):
        if n < len(from_x):
            share_one(upt_a, y_half, sem_upt_a, sem_mate_a, send_upt_mate.at[0], n, from_x[n])
        if n < len(from_y):
            share_one(upt_b, x_half, sem_upt_b, sem_mate_b, send_upt_mate.at[1], n, from_y[n])

    shared(upt_a, pl.ds((1 - core) * half_y, half_y), sem_mate_a, send_upt_mate.at[0], x, grid_x)
    contract(upt_a, hid_a, grad_a, gsend_a, grid_y)
    for k in far_first(grid_y):
        start(
            remote(gsend_a.at[y_peer(k)], grecv_a.at[y], send_grad.at[k], sem_grad_a.at[y], at_y(y_peer(k)))
        )
    shared(upt_b, pl.ds((1 - core) * half_x, half_x), sem_mate_b, send_upt_mate.at[1], y, grid_y)
    contract(upt_b, hid_b, grad_b, gsend_b, grid_x)
    for k in far_first(grid_x):
        start(
            remote(
                gsend_b.at[x_peer(k)], grecv_b.at[x], send_grad.at[grid_y + k], sem_grad_b.at[x], at_x(x_peer(k))
            )
        )

    def total_of(grad, grecv, sem, me, size, offset):
        value = grad[me]
        for other in arrivals(me, size):
            got = grecv.at[other]
            remote(got, got, send_grad.at[0], sem.at[other], mate).wait_recv()
            value = value + grecv[other].astype(F32)
        gradient[:, pl.ds(offset, cols)] = value

    total_of(grad_a, grecv_a, sem_grad_a, y, grid_y, 0)
    total_of(grad_b, grecv_b, sem_grad_b, x, grid_x, cols)
    outs.append(pltpu.make_async_copy(gradient, out_grad, sem_out.at[1]))
    outs[1].start()
    for copy in outs:
        copy.wait()
    for copy, when in sent:
        if when is None:
            copy.wait_send()
        else:
            pl.when(when)(copy.wait_send)


def on_device(grid_x, grid_y, chunks, *args):
    w_up, w_down, gate_act, hidden, block_input, norm_gain, loss_grad, moment_one, moment_two = args
    width, units = w_up.shape[1:]
    tokens = gate_act.shape[1]
    share = tokens // 4
    streams = 2
    stream = tokens // streams
    sub = stream // 4
    cols = units // 2
    row_share = width // (grid_x * grid_y)
    outs = [
        jax.ShapeDtypeStruct(block_input.shape, BF16),
        jax.ShapeDtypeStruct((row_share, units), F32),
    ]
    dma = pltpu.SemaphoreType.DMA
    vmem = pltpu.VMEM
    scratch = [
        vmem((width, units), BF16),
        vmem((width, units), BF16),
        vmem((tokens, units), BF16),
        vmem((share, width), BF16),
        vmem((1, width), F32),
        vmem((streams, stream, width), BF16),
        vmem((grid_x, grid_y, row_share, tokens), BF16),
        vmem((stream, units), F32),
        vmem((stream, units), BF16),
        vmem((streams, stream, width), F32),
        vmem((streams, stream, width), BF16),
        vmem((streams, 3, sub, width), BF16),
        vmem((sub, width), F32),
        vmem((share, width), BF16),
        vmem((grid_x, tokens, cols), BF16),
        vmem((grid_y, tokens, cols), BF16),
        vmem((grid_y, row_share, grid_x * tokens), BF16),
        vmem((grid_x, row_share, grid_y * tokens), BF16),
        vmem((grid_y, row_share, cols), F32),
        vmem((grid_x, row_share, cols), F32),
        vmem((grid_y, row_share, cols), BF16),
        vmem((grid_x, row_share, cols), BF16),
        vmem((grid_y, row_share, cols), BF16),
        vmem((grid_x, row_share, cols), BF16),
        vmem((row_share, units), F32),
        dma((6 + 12 * streams,)),
        dma((2,)),
        dma((streams, 2, chunks)),
        dma((streams, 2, chunks)),
        dma((streams, 3, chunks)),
        dma((grid_x,)),
        dma((grid_y,)),
        dma((grid_x,)),
        dma((grid_y,)),
        dma((grid_x,)),
        dma((grid_y,)),
        dma((grid_y,)),
        dma((grid_x,)),
        dma((streams, 2, chunks)),
        dma((streams, 2, chunks)),
        dma((streams, 3, chunks)),
        dma((streams, 2, chunks)),
        dma((grid_x + grid_y,)),
        dma((grid_x + grid_y,)),
        dma((2, max(grid_x, grid_y))),
        dma((grid_x + grid_y,)),
    ]
    anywhere = pl.BlockSpec(memory_space=pl.ANY)
    input_grad, gradient = pl.pallas_call(
        functools.partial(kernel, grid_x, grid_y, chunks),
        out_shape=outs,
        in_specs=[anywhere] * 7,
        out_specs=[anywhere] * 2,
        scratch_shapes=scratch,
        compiler_params=pltpu.CompilerParams(
            collective_id=0, has_side_effects=True, vmem_limit_bytes=67043328
        ),
    )(*args[:7])
    owner = lax.axis_index("dp")
    current = lax.dynamic_slice_in_dim(w_down[0], owner * row_share, row_share, 0).astype(F32)
    first = BETA_ONE * moment_one[0] + (1.0 - BETA_ONE) * gradient
    second = BETA_TWO * moment_two[0] + (1.0 - BETA_TWO) * gradient * gradient
    direction = first / CORRECT_ONE / (jnp.sqrt(second / CORRECT_TWO) + EPS_ADAM) + DECAY * current
    updated = current - RATE * direction
    return (input_grad, first[None], second[None], updated[None])


def solution(mesh, grid=(8, 8), chunks=2):
    in_specs = (
        P("pipe", None, "tensor"),
        P("pipe", None, "tensor"),
        P("pipe", "dp", "tensor"),
        P("pipe", "dp", "tensor"),
        P("pipe", ("dp", "tensor"), None),
        P("pipe", None),
        P(("dp", "tensor"), None),
        P("pipe", "dp", "tensor"),
        P("pipe", "dp", "tensor"),
    )
    out_specs = (
        P("pipe", ("dp", "tensor"), None),
        P("pipe", "dp", "tensor"),
        P("pipe", "dp", "tensor"),
        P("pipe", "dp", "tensor"),
    )
    return jax.shard_map(
        functools.partial(on_device, *grid, chunks),
        mesh=mesh, in_specs=in_specs, out_specs=out_specs, check_vma=False,
    )
```

```python
import functools

import jax
import jax.numpy as jnp
from jax import lax
from jax.experimental import pallas as pl
from jax.experimental.pallas import tpu as pltpu
from jax.sharding import PartitionSpec as P

EPS_NORM = 1e-05
EPS_ADAM = 1e-08
BETA_ONE = 0.9
BETA_TWO = 0.95
RATE = 0.01
DECAY = 0.1
CORRECT_ONE = 1.0 - 0.9**10
CORRECT_TWO = 1.0 - 0.95**10

MESH = pl.DeviceIdType.MESH
F32 = jnp.float32
BF16 = jnp.bfloat16


def far_first(size):
    return sorted(range(1, size), key=lambda k: -min(k, size - k))


def kernel(
    grid_x, grid_y, chunks,
    w_up, w_down, gate_act, hidden, block_input, norm_gain, loss_grad,
    out_dx, out_grad,
    wd, wu, gates, rows_in, gain,
    up, up_t, acc, unit, part, block_send, block_recv, scaled, dx,
    hid_a, hid_b, upt_a, upt_b, grad_a, grad_b, gsend_a, gsend_b, grecv_a, grecv_b, gradient,
    sem_in, sem_out, sem_block, sem_mate, sem_sum,
    sem_hid_a, sem_hid_b, sem_upt_a, sem_upt_b, sem_mate_a, sem_mate_b, sem_grad_a, sem_grad_b,
    send_fwd, send_mate, send_sum, send_dx,
    send_hid, send_upt, send_upt_mate, send_grad,
):
    pipe = lax.axis_index("pipe")
    owner = lax.axis_index("dp")
    tensor = lax.axis_index("tensor")
    sections = lax.axis_size("pipe")
    x = lax.div(owner, grid_y)
    y = lax.rem(owner, grid_y)
    chip = lax.div(tensor, 2)
    core = lax.rem(tensor, 2)
    mate = {"tensor": chip * 2 + 1 - core}
    across = {"tensor": (1 - chip) * 2 + core}
    last = pipe == sections - 1
    streams, stream, width = up.shape
    tokens = streams * stream
    share = tokens // 4
    sub = stream // 4
    units = wd.shape[1]
    row_share = width // (grid_x * grid_y)
    span = width // chunks
    cols = units // 2

    def x_peer(k):
        return lax.rem(x + k, grid_x)

    def y_peer(k):
        return lax.rem(y + k, grid_y)

    def at_x(index):
        return {"dp": index * grid_y + y}

    def at_y(index):
        return {"dp": x * grid_y + index}

    def aligned(value, step):
        return pl.multiple_of(value * step, step)

    def remote(src, dst, send, recv, device):
        return pltpu.make_async_remote_copy(
            src_ref=src, dst_ref=dst, send_sem=send, recv_sem=recv, device_id=device, device_id_type=MESH
        )

    sent = []
    targets = (1,)

    def start(copy, when=None):
        if when is None:
            copy.start()
        else:
            pl.when(when)(copy.start)
        sent.append((copy, when))

    order = [(s, c, z) for s in range(streams) for c in range(2) for z in range(2)]

    def token_rows(s, c, z):
        return pl.ds((z * 2 + c) * share + s * sub, sub)

    def stream_rows(s):
        return pl.ds(s * sub, sub)

    def columns(j):
        return pl.ds(j * span, span)

    loads = {}

    def load(name, src, dst, when=None):
        copy = pltpu.make_async_copy(src, dst, sem_in.at[len(loads)])
        loads[name] = copy
        if when is None:
            copy.start()
        else:
            pl.when(when)(copy.start)

    my_rows = pl.ds(aligned(core * 2 + chip, sub), sub)
    for s in range(streams):
        load(f"loss{s}", loss_grad.at[stream_rows(s)], up.at[s, my_rows], last)
    load("wd", w_down.at[0], wd)
    load("rows", block_input.at[0], rows_in)
    load("gain", norm_gain, gain)
    for n, key in enumerate(order):
        load(f"gate{n}", gate_act.at[0, token_rows(*key)], gates.at[pl.ds(n * sub, sub)])
    load("wu", w_up.at[0], wu)
    for n, key in enumerate(order):
        src = hidden.at[0, token_rows(*key)]
        load(f"hida{n}", src.at[:, pl.ds(0, cols)], hid_a.at[x, pl.ds(n * sub, sub)])
        load(f"hidb{n}", src.at[:, pl.ds(cols, cols)], hid_b.at[y, pl.ds(n * sub, sub)])

    others = [
        (across, core * 2 + 1 - chip),
        ({"tensor": (1 - chip) * 2 + 1 - core}, (1 - core) * 2 + 1 - chip),
        (mate, (1 - core) * 2 + chip),
    ]

    barrier = pltpu.get_barrier_semaphore()

    def greet(device):
        pl.semaphore_signal(barrier, inc=1, device_id=device, device_id_type=MESH)

    for k in far_first(grid_x):
        greet(at_x(x_peer(k)))
    for k in far_first(grid_y):
        greet(at_y(y_peer(k)))

    @pl.when(jnp.logical_and(pipe < sections - 1, chip == 1))
    def _():
        greet({"pipe": pipe + 1, "tensor": core})
        greet({"pipe": pipe + 1, "tensor": 2 + core})

    for device, _ in others:
        greet(device)

    @pl.when(pipe == 0)
    def _():
        pl.semaphore_wait(barrier, grid_x + grid_y + 1)

    @pl.when(pipe > 0)
    def _():
        pl.semaphore_wait(barrier, grid_x + grid_y + 2)

    @pl.when(last)
    def _():
        for s in range(streams):
            for j in range(chunks):
                remote(
                    loss_grad.at[stream_rows(s), columns(j)], up.at[s, my_rows, columns(j)],
                    send_fwd.at[s, chip, j], sem_block.at[s, chip, j], across,
                ).start()
        for s in range(streams):
            loads[f"loss{s}"].wait()

    for n in range(len(order)):
        loads[f"hida{n}"].wait()
        loads[f"hidb{n}"].wait()
    for k in far_first(grid_x):
        ref = hid_a.at[x]
        start(remote(ref, ref, send_hid.at[k], sem_hid_a.at[x], at_x(x_peer(k))))
    for k in far_first(grid_y):
        ref = hid_b.at[y]
        start(remote(ref, ref, send_hid.at[grid_x + k], sem_hid_b.at[y], at_y(y_peer(k))))

    loads["rows"].wait()
    source = rows_in[...].astype(F32)
    inverse_rms = lax.rsqrt(jnp.mean(source * source, axis=-1, keepdims=True) + EPS_NORM)
    for name in ("wd", "gain", "wu"):
        loads[name].wait()
    for n in range(len(order)):
        loads[f"gate{n}"].wait()

    def block(s, z, c, j):
        return up.at[s, pl.ds(aligned(c * 2 + z, sub), sub), columns(j)]

    def pass_on(s, j):
        for z in range(2):
            ref = block(s, z, core, j)
            forward = remote(ref, ref, send_fwd.at[s, z, j], sem_block.at[s, z, j], across)
            own = jnp.logical_and(last, chip == z)
            pl.when(jnp.logical_not(own))(forward.wait_recv)
            relay = jnp.logical_and(jnp.logical_not(last), chip == 1)
            pl.when(relay)(forward.start)
            sent.append((forward, jnp.logical_or(own, relay)))
            start(remote(ref, ref, send_mate.at[s, z, j], sem_mate.at[s, z, j], mate))

    def multiply(s, j):
        for z in range(2):
            ref = block(s, z, 1 - core, j)
            remote(ref, ref, send_mate.at[s, z, j], sem_mate.at[s, z, j], mate).wait_recv()
        left = up[s, :, columns(j)]
        for n in range(0, units, 256):
            right = pl.ds(n, 256)
            term = jnp.dot(left, wd[columns(j), right], preferred_element_type=F32)
            if j > 0:
                term = term + acc[:, right]
            if j < chunks - 1:
                acc[:, right] = term
            else:
                unit[:, right] = (term * gates[pl.ds(s * stream, stream), right].astype(F32)).astype(BF16)

    def sums(s, i):
        return [
            remote(
                block_send.at[s, pl.ds(aligned(row, sub), sub), columns(i)], block_recv.at[s, n, :, columns(i)],
                send_sum.at[s, n, i], sem_sum.at[s, n, i], device,
            )
            for n, (device, row) in enumerate(others)
        ]

    def second(s, i):
        for n in range(i * span, (i + 1) * span, 256):
            term = lax.dot_general(
                unit[...], wu[pl.ds(n, 256), :], (((1,), (1,)), ((), ())), preferred_element_type=F32
            )
            part[s, :, pl.ds(n, 256)] = term
            block_send[s, :, pl.ds(n, 256)] = term.astype(BF16)
        for copy in sums(s, i):
            start(copy)

    def finish(s):
        rows = stream_rows(s)
        scale = inverse_rms[s * sub : (s + 1) * sub]
        total = jnp.zeros((sub, 1), F32)
        for i in range(chunks):
            normed = part[s, my_rows, columns(i)]
            for n, copy in reversed(list(enumerate(sums(s, i)))):
                copy.wait_recv()
                normed = normed + block_recv[s, n, :, columns(i)].astype(F32)
            value = normed * gain[:, columns(i)]
            scaled[:, columns(i)] = value
            total = total + jnp.sum(rows_in[rows, columns(i)].astype(F32) * value, axis=-1, keepdims=True)
        slope = scale * scale * scale * (total / width)
        for i in range(chunks):
            dx[rows, columns(i)] = (
                up[s, my_rows, columns(i)].astype(F32)
                + scale * scaled[:, columns(i)]
                - rows_in[rows, columns(i)].astype(F32) * slope
            ).astype(BF16)
            for z in targets:
                start(
                    remote(
                        dx.at[rows, columns(i)], up.at[s, my_rows, columns(i)],
                        send_dx.at[s, z, i], sem_block.at[s, chip, i],
                        {"pipe": jnp.maximum(pipe - 1, 0), "tensor": z * 2 + core},
                    ),
                    pipe > 0,
                )

    half_y, half_x = grid_y // 2, grid_x // 2
    my_x, my_y = pl.ds(aligned(x, tokens), tokens), pl.ds(aligned(y, tokens), tokens)
    y_half, x_half = pl.ds(core * half_y, half_y), pl.ds(core * half_x, half_x)
    spread_a = [
        remote(
            up_t.at[x_peer(k), y_half], upt_a.at[y_half, :, my_x], send_upt.at[k], sem_upt_a.at[x], at_x(x_peer(k))
        )
        for k in far_first(grid_x)
    ]
    spread_b = [
        remote(
            up_t.at[x_half, y_peer(k)], upt_b.at[x_half, :, my_y], send_upt.at[grid_x + k], sem_upt_b.at[y],
            at_y(y_peer(k)),
        )
        for k in far_first(grid_y)
    ]

    quarters = 4 // chunks

    def turn(chunk):
        per = grid_x // 4
        for j in range(chunk * quarters, (chunk + 1) * quarters):
            wide = pl.ds(j * (width // 4), width // 4)
            turned = up[:, :, wide].reshape(tokens, width // 4).astype(F32).T.astype(BF16)
            if per:
                up_t[pl.ds(j * per, per)] = turned.reshape(per, grid_y, row_share, tokens)
            else:
                up_t[j // 2, pl.ds((j % 2) * half_y, half_y)] = turned.reshape(half_y, row_share, tokens)

    def spread():
        for n in range(max(grid_x, grid_y) - 1):
            for copies in (spread_a, spread_b):
                if n < len(copies):
                    copies[n].start()
        upt_a[:, :, my_x] = up_t[x]
        upt_b[:, :, my_y] = up_t[:, y]

    for s in range(streams):
        pass_on(s, 0)
        for j in range(chunks):
            if j + 1 < chunks:
                pass_on(s, j + 1)
            multiply(s, j)
            if s == streams - 1:
                pl.when(pipe == 0)(functools.partial(turn, j))
        if s == streams - 1:
            pl.when(pipe == 0)(spread)
        for i in range(chunks):
            second(s, i)
        if s > 0:
            finish(s - 1)
    finish(streams - 1)
    outs = [pltpu.make_async_copy(dx, out_dx.at[0], sem_out.at[0])]
    outs[0].start()

    @pl.when(pipe > 0)
    def _():
        for j in range(chunks):
            turn(j)
        spread()

    sent.extend((copy, None) for copy in spread_a + spread_b)

    def arrivals(me, size):
        return [lax.rem(me + size - k, size) for k in far_first(size)]

    def lane(slots, part_of, other):
        return slots.at[part_of, :, pl.ds(aligned(other, tokens), tokens)]

    def share_one(slots, mine, sem, mate_sem, send, n, other):
        ref = lane(slots, mine, other)
        copy = remote(ref, ref, send.at[n], sem.at[other], mate)
        copy.wait_recv()
        start(remote(ref, ref, send.at[n], mate_sem.at[other], mate))

    def shared(slots, theirs, mate_sem, send, me, size):
        for n, other in enumerate(arrivals(me, size)):
            ref = lane(slots, theirs, other)
            remote(ref, ref, send.at[n], mate_sem.at[other], mate).wait_recv()

    def gather_wait(slots, sem, me, size):
        for other in arrivals(me, size):
            got = slots.at[other]
            remote(got, got, send_hid.at[0], sem.at[other], mate).wait_recv()

    def contract(slots, hid, grad, gsend, size):
        left = slots[...].reshape(size * row_share, slots.shape[2])
        right = hid[...].reshape(hid.shape[0] * tokens, cols)
        for n in range(0, cols, 256):
            wide = min(256, cols)
            term = jnp.dot(left, right[:, n : n + wide], preferred_element_type=F32)
            term = term.reshape(size, row_share, wide)
            grad[:, :, pl.ds(n, wide)] = term
            gsend[:, :, pl.ds(n, wide)] = term.astype(BF16)

    gather_wait(hid_a, sem_hid_a, x, grid_x)
    gather_wait(hid_b, sem_hid_b, y, grid_y)
    from_x, from_y = arrivals(x, grid_x), arrivals(y, grid_y)
    for n in range(max(len(from_x), len(from_y))):
        if n < len(from_x):
            share_one(upt_a, y_half, sem_upt_a, sem_mate_a, send_upt_mate.at[0], n, from_x[n])
        if n < len(from_y):
            share_one(upt_b, x_half, sem_upt_b, sem_mate_b, send_upt_mate.at[1], n, from_y[n])

    shared(upt_a, pl.ds((1 - core) * half_y, half_y), sem_mate_a, send_upt_mate.at[0], x, grid_x)
    contract(upt_a, hid_a, grad_a, gsend_a, grid_y)
    for k in far_first(grid_y):
        start(
            remote(gsend_a.at[y_peer(k)], grecv_a.at[y], send_grad.at[k], sem_grad_a.at[y], at_y(y_peer(k)))
        )
    shared(upt_b, pl.ds((1 - core) * half_x, half_x), sem_mate_b, send_upt_mate.at[1], y, grid_y)
    contract(upt_b, hid_b, grad_b, gsend_b, grid_x)
    for k in far_first(grid_x):
        start(
            remote(
                gsend_b.at[x_peer(k)], grecv_b.at[x], send_grad.at[grid_y + k], sem_grad_b.at[x], at_x(x_peer(k))
            )
        )

    def total_of(grad, grecv, sem, me, size, offset):
        value = grad[me]
        for other in arrivals(me, size):
            got = grecv.at[other]
            remote(got, got, send_grad.at[0], sem.at[other], mate).wait_recv()
            value = value + grecv[other].astype(F32)
        part_of = pl.ds(offset, cols)
        gradient[:, part_of] = value
        copy = pltpu.make_async_copy(gradient.at[:, part_of], out_grad.at[:, part_of], sem_out.at[len(outs)])
        copy.start()
        outs.append(copy)

    total_of(grad_a, grecv_a, sem_grad_a, y, grid_y, 0)
    total_of(grad_b, grecv_b, sem_grad_b, x, grid_x, cols)
    for copy in outs:
        copy.wait()
    for copy, when in sent:
        if when is None:
            copy.wait_send()
        else:
            pl.when(when)(copy.wait_send)


def on_device(grid_x, grid_y, chunks, *args):
    w_up, w_down, gate_act, hidden, block_input, norm_gain, loss_grad, moment_one, moment_two = args
    width, units = w_up.shape[1:]
    tokens = gate_act.shape[1]
    share = tokens // 4
    streams = 2
    stream = tokens // streams
    sub = stream // 4
    cols = units // 2
    row_share = width // (grid_x * grid_y)
    outs = [
        jax.ShapeDtypeStruct(block_input.shape, BF16),
        jax.ShapeDtypeStruct((row_share, units), F32),
    ]
    dma = pltpu.SemaphoreType.DMA
    vmem = pltpu.VMEM
    scratch = [
        vmem((width, units), BF16),
        vmem((width, units), BF16),
        vmem((tokens, units), BF16),
        vmem((share, width), BF16),
        vmem((1, width), F32),
        vmem((streams, stream, width), BF16),
        vmem((grid_x, grid_y, row_share, tokens), BF16),
        vmem((stream, units), F32),
        vmem((stream, units), BF16),
        vmem((streams, stream, width), F32),
        vmem((streams, stream, width), BF16),
        vmem((streams, 3, sub, width), BF16),
        vmem((sub, width), F32),
        vmem((share, width), BF16),
        vmem((grid_x, tokens, cols), BF16),
        vmem((grid_y, tokens, cols), BF16),
        vmem((grid_y, row_share, grid_x * tokens), BF16),
        vmem((grid_x, row_share, grid_y * tokens), BF16),
        vmem((grid_y, row_share, cols), F32),
        vmem((grid_x, row_share, cols), F32),
        vmem((grid_y, row_share, cols), BF16),
        vmem((grid_x, row_share, cols), BF16),
        vmem((grid_y, row_share, cols), BF16),
        vmem((grid_x, row_share, cols), BF16),
        vmem((row_share, units), F32),
        dma((6 + 12 * streams,)),
        dma((3,)),
        dma((streams, 2, chunks)),
        dma((streams, 2, chunks)),
        dma((streams, 3, chunks)),
        dma((grid_x,)),
        dma((grid_y,)),
        dma((grid_x,)),
        dma((grid_y,)),
        dma((grid_x,)),
        dma((grid_y,)),
        dma((grid_y,)),
        dma((grid_x,)),
        dma((streams, 2, chunks)),
        dma((streams, 2, chunks)),
        dma((streams, 3, chunks)),
        dma((streams, 2, chunks)),
        dma((grid_x + grid_y,)),
        dma((grid_x + grid_y,)),
        dma((2, max(grid_x, grid_y))),
        dma((grid_x + grid_y,)),
    ]
    anywhere = pl.BlockSpec(memory_space=pl.ANY)
    input_grad, gradient = pl.pallas_call(
        functools.partial(kernel, grid_x, grid_y, chunks),
        out_shape=outs,
        in_specs=[anywhere] * 7,
        out_specs=[anywhere] * 2,
        scratch_shapes=scratch,
        compiler_params=pltpu.CompilerParams(
            collective_id=0, has_side_effects=True, vmem_limit_bytes=48 * 1024 * 1024
        ),
    )(*[pltpu.with_memory_space_constraint(a, pltpu.HBM) for a in args[:7]])
    owner = lax.axis_index("dp")
    current = lax.dynamic_slice_in_dim(w_down[0], owner * row_share, row_share, 0).astype(F32)
    first = BETA_ONE * moment_one[0] + (1.0 - BETA_ONE) * gradient
    second = BETA_TWO * moment_two[0] + (1.0 - BETA_TWO) * gradient * gradient
    direction = first / CORRECT_ONE / (jnp.sqrt(second / CORRECT_TWO) + EPS_ADAM) + DECAY * current
    updated = current - RATE * direction
    return (input_grad, first[None], second[None], updated[None])


def solution(mesh, grid=(8, 8), chunks=2):
    in_specs = (
        P("pipe", None, "tensor"),
        P("pipe", None, "tensor"),
        P("pipe", "dp", "tensor"),
        P("pipe", "dp", "tensor"),
        P("pipe", ("dp", "tensor"), None),
        P("pipe", None),
        P(("dp", "tensor"), None),
        P("pipe", "dp", "tensor"),
        P("pipe", "dp", "tensor"),
    )
    out_specs = (
        P("pipe", ("dp", "tensor"), None),
        P("pipe", "dp", "tensor"),
        P("pipe", "dp", "tensor"),
        P("pipe", "dp", "tensor"),
    )
    return jax.shard_map(
        functools.partial(on_device, *grid, chunks),
        mesh=mesh, in_specs=in_specs, out_specs=out_specs, check_vma=False,
    )
```
